32 devices in a mesh: grp: 2 (over x), row: 16 (over z, y, core).
Axes of the slice: x: 2, y: 2, z: 4, core: 2. Of those that a mesh axis runs over, the one named last changes fastest.
Arguments:
- excitations: bfloat16 [32, 8192, 128], P('grp', 'row'), parts along dimension 0, may hold values from -0.005859375 to 0.005859375
- valence_orb: bfloat16 [2048, 128], P(('grp', 'row')), parts along dimension 0, may hold values from -6 to 6
- conduction_orb: bfloat16 [2048, 8192], P(('grp', 'row')), parts along dimension 0, may hold values from -6 to 6
- screened: bfloat16 [2048, 1024], P(('grp', 'row')), parts along dimension 0, may hold values from -0.005859375 to 0.005859375
Outputs:
- action: bfloat16 [32, 8192, 128], P('grp', 'row'), parts along dimension 0
The draws below stay inside these ranges and needn't reach their ends.
There are 2 independent parts, one for each index of `grp`. The reference program is written for one: setup_inputs(seed, part) draws one part's arguments, and reference() takes and returns one part's arrays. A program takes and returns all parts, laid end to end along the dimension named above; each array names one. Nothing has to cross between parts.
All inputs are finite; a program needn't handle non-finite values.
Results may differ from the reference program's by a relative error of at most 0.0064.
Values may be sent and summed in bfloat16 or wider, within the bound.
A program may use at most 64 MiB of HBM per device.

```python
import math
import jax
import jax.numpy as jnp
from jax import lax

B = 16
V = 128
C = 8192
P_SIZE = 1024


def shard_levels(own_key, shape, cuts, smallest, high):
    factor_of, own = 1.0, jax.random.fold_in(own_key, 6)
    for axis_at, blocks in cuts:
        heights = jnp.exp(jax.random.uniform(jax.random.fold_in(own, axis_at), (blocks,), jnp.float32, smallest / len(cuts), high / len(cuts)))
        factor_of = factor_of * jnp.repeat(heights, shape[axis_at] // blocks).reshape([-1 if axis == axis_at else 1 for axis in range(len(shape))])
    return factor_of


def gaussian(stream_key, extent, width, bound, pieces=(), held_as=jnp.bfloat16):
    factor_of = shard_levels(stream_key, extent, pieces, -0.22, 0.18) if pieces else 1.0
    drawn = jax.random.normal(stream_key, extent, jnp.float32) * width * factor_of
    return jnp.minimum(jnp.maximum(drawn, -bound), bound).astype(held_as)


def setup_inputs(seed: int = 0, part: int = 0) -> dict:
    arg_keys = jax.random.split(jax.random.key(seed), 5)
    part_keys = jax.random.split(jax.random.fold_in(arg_keys[4], part), 5)
    excitations = gaussian(part_keys[0], (B, C, V), (V * C) ** -0.5, 0.005859375, ((1, 16),))
    valence_orb = gaussian(part_keys[1], (P_SIZE, V), 1.0, 6.0, ((0, 16),))
    conduction_orb = gaussian(part_keys[2], (P_SIZE, C), 1.0, 6.0, ((0, 16),))
    screened = gaussian(part_keys[3], (P_SIZE, P_SIZE), (P_SIZE * P_SIZE) ** -0.5, 0.005859375, ((0, 16),))
    return {"excitations": excitations, "valence_orb": valence_orb, "conduction_orb": conduction_orb, "screened": screened}


def reference(excitations, valence_orb, conduction_orb, screened):
    span_size = math.gcd(P_SIZE, 512)
    block_count = P_SIZE // span_size
    exc = excitations.astype(jnp.float32)
    val_blocks = valence_orb.reshape(block_count, span_size, V)
    cond_blocks = conduction_orb.reshape(block_count, span_size, C)

    def density_block(blocks):
        val_block, cond_block = blocks
        mixed = jnp.einsum("bcv,mv->bmc", exc, val_block.astype(jnp.float32))
        return jnp.sum(mixed * cond_block.astype(jnp.float32)[None], axis=2)

    density = lax.map(density_block, (val_blocks, cond_blocks))
    density = density.transpose(1, 0, 2).reshape(B, P_SIZE).astype(jnp.bfloat16)
    field = jnp.dot(density, screened.T, preferred_element_type=jnp.float32).astype(jnp.bfloat16)
    field_blocks = field.reshape(B, block_count, span_size).transpose(1, 0, 2)

    def project(total, blocks):
        val_block, cond_block, field_block = blocks
        pair = (cond_block.astype(jnp.float32)[None] * field_block.astype(jnp.float32)[:, :, None]).astype(jnp.bfloat16)
        pair = lax.optimization_barrier(pair).astype(jnp.float32)
        total = total + jnp.einsum("bmc,mv->bcv", pair, val_block.astype(jnp.float32))
        return total, None

    initial = jnp.zeros((B, C, V), jnp.float32)
    total, unused = lax.scan(project, initial, (val_blocks, cond_blocks, field_blocks))
    return total.astype(jnp.bfloat16)
```

```python
import functools
import math

import jax
import jax.numpy as jnp
from jax import lax
from jax.experimental import pallas as pl
from jax.experimental.pallas import tpu as pltpu
from jax.sharding import PartitionSpec as P

MESH = pl.DeviceIdType.MESH
NT = (((1,), (1,)), ((), ()))


def flip(index, other, bits):
    total = 0
    for bit in range(bits):
        a = (index // (1 << bit)) % 2
        b = (other // (1 << bit)) % 2
        total = total + (a + b - 2 * a * b) * (1 << bit)
    return total


def gather_kernel(
    n, planes,
    exc_hbm, val_ref, cond_hbm, scr_ref,
    condt_ref, valt_ref, field_ref,
    exc, exct, cond_all, val_all, scr_chip, part, red, dens, dens_all, fld, fld_all,
    exc_sem, own_sem,
    cond_send, cond_recv, scr_send, scr_recv, va_send, va_recv, vb_send, vb_recv,
    part_send, part_recv, dens_send, dens_recv, fld_send, fld_recv,
):
    rows, cl = val_ref.shape[0], exc.shape[1]
    batch = exc.shape[0]
    half = batch // 2
    q = n // planes
    bits = n.bit_length() - 1
    chips = n // 2
    me = lax.axis_index("row")
    my_z, my_q = me // q, me % q
    chip, core = me // 2, me % 2

    exc_copy = pltpu.make_async_copy(exc_hbm, exc, exc_sem)
    exc_copy.start()
    own_val = pltpu.make_async_copy(val_ref, val_all.at[my_q, my_z], own_sem.at[0])
    own_val.start()
    own_scr = pltpu.make_async_copy(scr_ref, scr_chip.at[core], own_sem.at[1])
    own_scr.start()
    pltpu.make_async_copy(
        cond_hbm.at[:, pl.ds(pl.multiple_of(me * cl, cl), cl)], cond_all.at[me], cond_recv.at[me]
    ).start()

    barrier = pltpu.get_barrier_semaphore()
    for k in range(1, n):
        pl.semaphore_signal(barrier, inc=1, device_id={"row": flip(me, k, bits)}, device_id_type=MESH)
    pl.semaphore_wait(barrier, n - 1)

    def remote(src, dst, send, recv, to):
        return pltpu.make_async_remote_copy(
            src_ref=src, dst_ref=dst, send_sem=send, recv_sem=recv,
            device_id={"row": to}, device_id_type=MESH,
        )

    sent = []
    zbits, qbits = planes.bit_length() - 1, q.bit_length() - 1
    for k in range(planes - 1, 0, -1):
        to = flip(my_z, k, zbits) * q + my_q
        copy = remote(val_ref, val_all.at[my_q, my_z], va_send.at[k], va_recv.at[my_z], to)
        copy.start()
        sent.append(copy)
    for k in range(n - 1, 0, -1):
        to = flip(me, k, bits)
        copy = remote(
            cond_hbm.at[:, pl.ds(pl.multiple_of(to * cl, cl), cl)], cond_all.at[me],
            cond_send.at[k], cond_recv.at[me], to,
        )
        copy.start()
        sent.append(copy)
    copy = remote(scr_ref, scr_chip.at[core], scr_send, scr_recv, chip * 2 + 1 - core)
    copy.start()
    sent.append(copy)

    exc_copy.wait()

    def turn(b, carry):
        exct[pl.ds(pl.multiple_of(b * 128, 128), 128), :] = exc[b].T
        return carry

    lax.fori_loop(0, batch, turn, 0)

    own_val.wait()
    for k in range(1, planes):
        z = flip(my_z, k, zbits)
        pltpu.make_async_copy(val_ref, val_all.at[my_q, z], va_recv.at[z]).wait()
    for k in range(1, q):
        to = my_z * q + flip(my_q, k, qbits)
        copy = remote(val_all.at[my_q], val_all.at[my_q], vb_send.at[k], vb_recv.at[my_q], to)
        copy.start()
        sent.append(copy)
    for k in range(1, q):
        other = flip(my_q, k, qbits)
        pltpu.make_async_copy(val_all.at[other], val_all.at[other], vb_recv.at[other]).wait()

    def group(k, carry):
        p = flip(chip, k, bits - 1)
        z, y = p // (q // 2), p % (q // 2)
        lanes = pl.ds(pl.multiple_of(p * 2 * rows, 2 * rows), 2 * rows)
        for h in range(2):
            pltpu.make_async_copy(cond_all.at[2 * p + h], cond_all.at[2 * p + h], cond_recv.at[2 * p + h]).wait()
        block = cond_all[pl.ds(2 * p, 2)].reshape(2 * rows, cl)
        vals = jnp.concatenate([val_all[2 * y, z], val_all[2 * y + 1, z]], axis=0)
        valt = vals.astype(jnp.float32).T
        valt_ref[:, lanes] = valt.astype(jnp.bfloat16)
        mixed = lax.dot_general(exct[...], block, NT, preferred_element_type=jnp.float32)
        summed = jnp.sum(mixed.reshape(batch, valt.shape[0], 2 * rows) * valt[None], axis=1)
        part[k, 0] = summed[:half]
        part[k, 1] = summed[half:]

        @pl.when(k == 0)
        def _():
            remote(
                part.at[k, 1 - core], red.at[me], part_send.at[k, 1 - core], part_recv.at[me],
                2 * chip + 1 - core,
            ).start()
            red[me] = part[0, core]

        @pl.when(k > 0)
        def _():
            for h in range(2):
                remote(
                    part.at[k, h], red.at[me], part_send.at[k, h], part_recv.at[me], 2 * p + h
                ).start()

        condt_ref[:, lanes] = block.T
        return carry

    lax.fori_loop(0, chips, group, 0)

    own_scr.wait()
    pltpu.make_async_copy(scr_chip.at[1 - core], scr_chip.at[1 - core], scr_recv).wait()
    total = red[me]
    for k in range(1, n):
        other = flip(me, k, bits)
        pltpu.make_async_copy(red.at[other], red.at[other], part_recv.at[other]).wait()
        total = total + red[other]
    dens[...] = total.astype(jnp.bfloat16)
    dens_all[chip] = total.astype(jnp.bfloat16)
    for k in range(chips - 1, 0, -1):
        to = flip(chip, k, bits - 1)
        copy = remote(dens, dens_all.at[chip], dens_send.at[k], dens_recv.at[chip], 2 * to + core)
        copy.start()
        sent.append(copy)
    for k in range(1, chips):
        other = flip(chip, k, bits - 1)
        pltpu.make_async_copy(dens_all.at[other], dens_all.at[other], dens_recv.at[other]).wait()
    whole = jnp.concatenate([dens_all[p].astype(jnp.float32) for p in range(chips)], axis=1).astype(jnp.bfloat16)
    screened = scr_chip[...].reshape(2 * rows, scr_ref.shape[1])
    mine = lax.dot_general(whole, screened, NT, preferred_element_type=jnp.float32).astype(jnp.bfloat16)
    fld[...] = mine
    fld_all[me] = mine
    for k in range(n - 1, 0, -1):
        copy = remote(fld, fld_all.at[me], fld_send.at[k], fld_recv.at[me], flip(me, k, bits))
        copy.start()
        sent.append(copy)
    for k in range(1, n):
        other = flip(me, k, bits)
        pltpu.make_async_copy(fld_all.at[other], fld_all.at[other], fld_recv.at[other]).wait()
    for p in range(chips):
        for h in range(2):
            field_ref[h * half:(h + 1) * half, p * 2 * rows:(p + 1) * 2 * rows] = fld_all[2 * p + h].astype(jnp.float32)

    for copy in sent:
        copy.wait_send()
    remote(
        part.at[0, 1 - core], red.at[me], part_send.at[0, 1 - core], part_recv.at[me], 2 * chip + 1 - core
    ).wait_send()
    for k in range(1, chips):
        p = flip(chip, k, bits - 1)
        for h in range(2):
            remote(part.at[k, h], red.at[me], part_send.at[k, h], part_recv.at[me], 2 * p + h).wait_send()


def project_kernel(per, condt_ref, valt_ref, field_ref, out_ref):
    step = pl.program_id(0)
    v = valt_ref.shape[0]
    valt = valt_ref[...].astype(jnp.float32)
    for j in range(0, per, 2):
        weights = jnp.concatenate(
            [(valt * field_ref[pl.ds(step * per + j + i, 1), :]).astype(jnp.bfloat16) for i in range(2)], axis=0
        )
        summed = lax.dot_general(condt_ref[...], weights, NT, preferred_element_type=jnp.float32)
        for i in range(2):
            out_ref[j + i] = summed[:, i * v:(i + 1) * v].astype(jnp.bfloat16)


def fast_body(n, excitations, valence_orb, conduction_orb, screened):
    batch, cl, v = excitations.shape
    rows, points = screened.shape
    planes = 4 if n % 8 == 0 else 2
    q, chips, half = n // planes, n // 2, batch // 2
    bf, f32 = jnp.bfloat16, jnp.float32
    any_ = pl.BlockSpec(memory_space=pl.ANY)
    vmem = pl.BlockSpec(memory_space=pltpu.VMEM)
    dma = pltpu.SemaphoreType.DMA
    condt, valt, field = pl.pallas_call(
        functools.partial(gather_kernel, n, planes),
        out_shape=(
            jax.ShapeDtypeStruct((cl, points), bf),
            jax.ShapeDtypeStruct((v, points), bf),
            jax.ShapeDtypeStruct((batch, points), f32),
        ),
        in_specs=[any_, vmem, any_, vmem],
        out_specs=(vmem, vmem, vmem),
        scratch_shapes=[
            pltpu.VMEM((batch, cl, v), bf),
            pltpu.VMEM((batch * v, cl), bf),
            pltpu.VMEM((n, rows, cl), bf),
            pltpu.VMEM((q, planes, rows, v), bf),
            pltpu.VMEM((2, rows, points), bf),
            pltpu.VMEM((chips, 2, half, 2 * rows), f32),
            pltpu.VMEM((n, half, 2 * rows), f32),
            pltpu.VMEM((half, 2 * rows), bf),
            pltpu.VMEM((chips, half, 2 * rows), bf),
            pltpu.VMEM((half, 2 * rows), bf),
            pltpu.VMEM((n, half, 2 * rows), bf),
            dma, dma((2,)),
            dma((n,)), dma((n,)), dma, dma, dma((planes,)), dma((planes,)), dma((q,)), dma((q,)),
            dma((chips, 2)), dma((n,)), dma((chips,)), dma((chips,)), dma((n,)), dma((n,)),
        ],
        compiler_params=pltpu.CompilerParams(
            collective_id=0, has_side_effects=True, vmem_limit_bytes=40 * 1024 * 1024
        ),
        name="gather_field",
    )(excitations, valence_orb, conduction_orb, screened)
    per = 4
    whole = lambda i: (0, 0)
    return pl.pallas_call(
        functools.partial(project_kernel, per),
        grid=(batch // per,),
        out_shape=jax.ShapeDtypeStruct((batch, cl, v), bf),
        in_specs=[
            pl.BlockSpec((cl, points), whole),
            pl.BlockSpec((v, points), whole),
            pl.BlockSpec((batch, points), whole),
        ],
        out_specs=pl.BlockSpec((per, cl, v), lambda i: (i, 0, 0)),
        name="project",
    )(condt, valt, field)


def over_blocks(total_rows, step_fn, initial):
    span_size = math.gcd(total_rows, 2048)
    block_count = total_rows // span_size
    if block_count == 1:
        return step_fn(initial, 0, span_size)
    return lax.fori_loop(
        0, block_count, lambda index, carry: step_fn(carry, index * span_size, span_size), initial
    )


def density_rows(flat_exc, batch, valence_rows, cond_rows):
    total_rows = valence_rows.shape[0]
    cond_local = cond_rows.shape[1]
    initial = jnp.zeros((batch, total_rows), jnp.float32)

    def step_fn(carry, offset, span_size):
        val_block = lax.dynamic_slice_in_dim(valence_rows, offset, span_size, 0)
        cond_block = lax.dynamic_slice_in_dim(cond_rows, offset, span_size, 0)
        mixed = lax.dot_general(
            flat_exc, val_block, (((1,), (1,)), ((), ())), preferred_element_type=jnp.float32
        )
        mixed = mixed.reshape(batch, cond_local, span_size)
        summed = jnp.sum(mixed * cond_block.T.astype(jnp.float32)[None], axis=1)
        return lax.dynamic_update_slice_in_dim(carry, summed, offset, 1)

    return over_blocks(total_rows, step_fn, initial)


def projection(carry, valence_rows, cond_rows, field_cols):
    total_rows = valence_rows.shape[0]
    batch = field_cols.shape[0]
    cond_local = cond_rows.shape[1]

    def step_fn(inner, offset, span_size):
        val_block = lax.dynamic_slice_in_dim(valence_rows, offset, span_size, 0)
        cond_block = lax.dynamic_slice_in_dim(cond_rows, offset, span_size, 0)
        field_block = lax.dynamic_slice_in_dim(field_cols, offset, span_size, 1)
        pair = (
            cond_block.T.astype(jnp.float32)[None] * field_block.astype(jnp.float32)[:, None, :]
        ).astype(jnp.bfloat16)
        pair = pair.reshape(batch * cond_local, span_size)
        return inner + jnp.dot(pair, val_block, preferred_element_type=jnp.float32)

    return over_blocks(total_rows, step_fn, carry)


def general_body(excitations, valence_orb, conduction_orb, screened):
    batch, cond_local, valence = excitations.shape
    flat_exc = excitations.reshape(batch * cond_local, valence)
    valence_whole = lax.all_gather(valence_orb, "row", axis=0, tiled=True)
    cond_rows = lax.all_to_all(conduction_orb, "row", split_axis=1, concat_axis=0, tiled=True)
    partial_density = density_rows(flat_exc, batch, valence_whole, cond_rows)
    density_whole = lax.psum(partial_density, "row").astype(jnp.bfloat16)
    field_mine = lax.dot_general(
        density_whole, screened, (((1,), (1,)), ((), ())), preferred_element_type=jnp.float32
    ).astype(jnp.bfloat16)
    initial = jnp.zeros((batch * cond_local, valence), jnp.float32)
    summed = projection(
        initial, valence_whole, cond_rows, lax.all_gather(field_mine, "row", axis=1, tiled=True)
    )
    return summed.reshape(batch, cond_local, valence).astype(jnp.bfloat16)


def body(n, excitations, valence_orb, conduction_orb, screened):
    batch, cl, v = excitations.shape
    rows = valence_orb.shape[0]
    fits = n in (8, 16) and cl % 128 == 0 and v == 128 and rows == 64 and batch == 16
    if fits:
        return fast_body(n, excitations, valence_orb, conduction_orb, screened)
    return general_body(excitations, valence_orb, conduction_orb, screened)


def solution(mesh):
    in_specs = (
        P("grp", "row", None),
        P(("grp", "row"), None),
        P(("grp", "row"), None),
        P(("grp", "row"), None),
    )
    out_specs = P("grp", "row", None)
    return jax.shard_map(
        functools.partial(body, mesh.shape["row"]),
        mesh=mesh, in_specs=in_specs, out_specs=out_specs, check_vma=False,
    )
```

```python
import functools
import math

import jax
import jax.numpy as jnp
from jax import lax
from jax.experimental import pallas as pl
from jax.experimental.pallas import tpu as pltpu
from jax.sharding import PartitionSpec as P

MESH = pl.DeviceIdType.MESH
NT = (((1,), (1,)), ((), ()))


def flip(index, other, bits):
    total = 0
    for bit in range(bits):
        a = (index // (1 << bit)) % 2
        b = (other // (1 << bit)) % 2
        total = total + (a + b - 2 * a * b) * (1 << bit)
    return total


def send_order(n, q):
    far = list(range(n - 1, n // 2 - 1, -1))
    near = [1] + [k for k in range(n // 2 - 1, 1, -1) if k // 2 != q // 4]
    near[3:3] = [k for k in range(n // 2 - 1, 1, -1) if k // 2 == q // 4]
    order = []
    while far or near:
        order += far[:2] + near[:3]
        far, near = far[2:], near[3:]
    return order


def work_order(n, q):
    seen, order = {0}, [0]
    for k in send_order(n, q):
        seen.add(k)
        if seen >= {k, k ^ 1} and k // 2 not in order:
            order.append(k // 2)
    return order


def gather_kernel(
    n, planes,
    exc_hbm, val_ref, cond_hbm, scr_ref,
    condt_hbm, valt_hbm, field_hbm,
    condt_ref, valt_ref, field_ref, exc, exct, cond_all, val_all, scr_chip, part, red, dens, dens_all, fld, fld_all,
    exc_sem, own_sem, out_sem, field_sem,
    cond_send, cond_recv, scr_send, scr_recv, va_send, va_recv, vb_send, vb_recv,
    part_send, part_recv, dens_send, dens_recv, fld_send, fld_recv,
):
    rows, cl = val_ref.shape[0], exc.shape[1]
    batch = exc.shape[0]
    half = batch // 2
    q = n // planes
    bits = n.bit_length() - 1
    chips = n // 2
    me = lax.axis_index("row")
    my_z, my_q = me // q, me % q
    chip, core = me // 2, me % 2

    exc_copy = pltpu.make_async_copy(exc_hbm, exc, exc_sem)
    exc_copy.start()
    own_val = pltpu.make_async_copy(val_ref, val_all.at[my_q, my_z], own_sem.at[0])
    own_val.start()
    own_scr = pltpu.make_async_copy(scr_ref, scr_chip.at[core], own_sem.at[1])
    own_scr.start()
    pltpu.make_async_copy(
        cond_hbm.at[:, pl.ds(pl.multiple_of(me * cl, cl), cl)], cond_all.at[me], cond_recv.at[me]
    ).start()

    barrier = pltpu.get_barrier_semaphore()
    for k in range(1, n):
        pl.semaphore_signal(barrier, inc=1, device_id={"row": flip(me, k, bits)}, device_id_type=MESH)
    pl.semaphore_wait(barrier, n - 1)

    def remote(src, dst, send, recv, to):
        return pltpu.make_async_remote_copy(
            src_ref=src, dst_ref=dst, send_sem=send, recv_sem=recv,
            device_id={"row": to}, device_id_type=MESH,
        )

    sent = []
    zbits, qbits = planes.bit_length() - 1, q.bit_length() - 1
    for k in range(planes - 1, 0, -1):
        to = flip(my_z, k, zbits) * q + my_q
        copy = remote(val_ref, val_all.at[my_q, my_z], va_send.at[k], va_recv.at[my_z], to)
        copy.start()
        sent.append(copy)
    for k in send_order(n, q):
        to = flip(me, k, bits)
        copy = remote(
            cond_hbm.at[:, pl.ds(pl.multiple_of(to * cl, cl), cl)], cond_all.at[me],
            cond_send.at[k], cond_recv.at[me], to,
        )
        copy.start()
        sent.append(copy)
    copy = remote(scr_ref, scr_chip.at[core], scr_send, scr_recv, chip * 2 + 1 - core)
    copy.start()
    sent.append(copy)

    exc_copy.wait()

    def turn(b, carry):
        exct[pl.ds(pl.multiple_of(b * 128, 128), 128), :] = exc[b].T
        return carry

    lax.fori_loop(0, batch, turn, 0)

    own_val.wait()
    for k in range(1, planes):
        z = flip(my_z, k, zbits)
        pltpu.make_async_copy(val_ref, val_all.at[my_q, z], va_recv.at[z]).wait()
    for k in range(1, q):
        to = my_z * q + flip(my_q, k, qbits)
        copy = remote(val_all.at[my_q], val_all.at[my_q], vb_send.at[k], vb_recv.at[my_q], to)
        copy.start()
        sent.append(copy)
    for k in range(1, q):
        other = flip(my_q, k, qbits)
        pltpu.make_async_copy(val_all.at[other], val_all.at[other], vb_recv.at[other]).wait()

    def group(step, carry):
        k = 0
        for at, value in enumerate(work_order(n, q)):
            k = k + jnp.where(step == at, value, 0)
        p = flip(chip, k, bits - 1)
        z, y = p // (q // 2), p % (q // 2)
        lanes = pl.ds(pl.multiple_of(p * 2 * rows, 2 * rows), 2 * rows)
        for h in range(2):
            pltpu.make_async_copy(cond_all.at[2 * p + h], cond_all.at[2 * p + h], cond_recv.at[2 * p + h]).wait()
        block = cond_all[pl.ds(2 * p, 2)].reshape(2 * rows, cl)
        vals = jnp.concatenate([val_all[2 * y, z], val_all[2 * y + 1, z]], axis=0)
        valt = vals.astype(jnp.float32).T
        valt_ref[:, lanes] = valt.astype(jnp.bfloat16)
        mixed = lax.dot_general(exct[...], block, NT, preferred_element_type=jnp.float32)
        summed = jnp.sum(mixed.reshape(batch, valt.shape[0], 2 * rows) * valt[None], axis=1)
        part[k, 0] = summed[:half]
        part[k, 1] = summed[half:]

        @pl.when(k == 0)
        def _():
            remote(
                part.at[k, 1 - core], red.at[me], part_send.at[k, 1 - core], part_recv.at[me],
                2 * chip + 1 - core,
            ).start()
            red[me] = part[0, core]

        @pl.when(k > 0)
        def _():
            for h in range(2):
                remote(
                    part.at[k, h], red.at[me], part_send.at[k, h], part_recv.at[me], 2 * p + h
                ).start()

        condt_ref[:, lanes] = block.T
        pltpu.make_async_copy(condt_ref.at[:, lanes], condt_hbm.at[:, lanes], out_sem.at[k, 0]).start()
        pltpu.make_async_copy(valt_ref.at[:, lanes], valt_hbm.at[:, lanes], out_sem.at[k, 1]).start()
        return carry

    lax.fori_loop(0, chips, group, 0)

    own_scr.wait()
    pltpu.make_async_copy(scr_chip.at[1 - core], scr_chip.at[1 - core], scr_recv).wait()
    total = red[me]
    for k in range(1, n):
        other = flip(me, k, bits)
        pltpu.make_async_copy(red.at[other], red.at[other], part_recv.at[other]).wait()
        total = total + red[other]
    dens[...] = total.astype(jnp.bfloat16)
    dens_all[chip] = total.astype(jnp.bfloat16)
    for k in range(chips - 1, 0, -1):
        to = flip(chip, k, bits - 1)
        copy = remote(dens, dens_all.at[chip], dens_send.at[k], dens_recv.at[chip], 2 * to + core)
        copy.start()
        sent.append(copy)
    for k in range(1, chips):
        other = flip(chip, k, bits - 1)
        pltpu.make_async_copy(dens_all.at[other], dens_all.at[other], dens_recv.at[other]).wait()
    whole = jnp.concatenate([dens_all[p].astype(jnp.float32) for p in range(chips)], axis=1).astype(jnp.bfloat16)
    screened = scr_chip[...].reshape(2 * rows, scr_ref.shape[1])
    mine = lax.dot_general(whole, screened, NT, preferred_element_type=jnp.float32).astype(jnp.bfloat16)
    fld[...] = mine
    fld_all[me] = mine
    for k in range(n - 1, 0, -1):
        copy = remote(fld, fld_all.at[me], fld_send.at[k], fld_recv.at[me], flip(me, k, bits))
        copy.start()
        sent.append(copy)
    for k in range(1, n):
        other = flip(me, k, bits)
        pltpu.make_async_copy(fld_all.at[other], fld_all.at[other], fld_recv.at[other]).wait()
    for p in range(chips):
        for h in range(2):
            field_ref[h * half:(h + 1) * half, p * 2 * rows:(p + 1) * 2 * rows] = fld_all[2 * p + h].astype(jnp.float32)

    field_copy = pltpu.make_async_copy(field_ref, field_hbm, field_sem)
    field_copy.start()
    for k in range(chips):
        lanes = pl.ds(pl.multiple_of(flip(chip, k, bits - 1) * 2 * rows, 2 * rows), 2 * rows)
        pltpu.make_async_copy(condt_ref.at[:, lanes], condt_hbm.at[:, lanes], out_sem.at[k, 0]).wait()
        pltpu.make_async_copy(valt_ref.at[:, lanes], valt_hbm.at[:, lanes], out_sem.at[k, 1]).wait()
    field_copy.wait()

    for copy in sent:
        copy.wait_send()
    remote(
        part.at[0, 1 - core], red.at[me], part_send.at[0, 1 - core], part_recv.at[me], 2 * chip + 1 - core
    ).wait_send()
    for k in range(1, chips):
        p = flip(chip, k, bits - 1)
        for h in range(2):
            remote(part.at[k, h], red.at[me], part_send.at[k, h], part_recv.at[me], 2 * p + h).wait_send()


def project_kernel(condt_hbm, valt_hbm, field_hbm, out_hbm, condt_ref, valt_ref, field_ref, held, in_sem, out_sem):
    loads = [
        pltpu.make_async_copy(src, dst, in_sem.at[at])
        for at, (src, dst) in enumerate(((valt_hbm, valt_ref), (field_hbm, field_ref), (condt_hbm, condt_ref)))
    ]
    for load in loads:
        load.start()
    loads[0].wait()
    loads[1].wait()
    v = valt_ref.shape[0]
    batch = field_ref.shape[0]
    valt = valt_ref[...].astype(jnp.float32)
    copies = []
    for b in range(0, batch, 2):
        weights = jnp.concatenate(
            [(valt * field_ref[b + i:b + i + 1, :]).astype(jnp.bfloat16) for i in range(2)], axis=0
        )
        if b == 0:
            loads[2].wait()
        summed = lax.dot_general(condt_ref[...], weights, NT, preferred_element_type=jnp.float32)
        for i in range(2):
            held[b + i] = summed[:, i * v:(i + 1) * v].astype(jnp.bfloat16)
        copy = pltpu.make_async_copy(held.at[pl.ds(b, 2)], out_hbm.at[pl.ds(b, 2)], out_sem.at[b // 2])
        copy.start()
        copies.append(copy)
    for copy in copies:
        copy.wait()


def fast_body(n, excitations, valence_orb, conduction_orb, screened):
    batch, cl, v = excitations.shape
    rows, points = screened.shape
    planes = 4 if n % 8 == 0 else 2
    q, chips, half = n // planes, n // 2, batch // 2
    bf, f32 = jnp.bfloat16, jnp.float32
    hbm = pl.BlockSpec(memory_space=pltpu.HBM)
    dma = pltpu.SemaphoreType.DMA
    condt, valt, field = pl.pallas_call(
        functools.partial(gather_kernel, n, planes),
        out_shape=(
            jax.ShapeDtypeStruct((cl, points), bf),
            jax.ShapeDtypeStruct((v, points), bf),
            jax.ShapeDtypeStruct((batch, points), f32),
        ),
        in_specs=[hbm, hbm, hbm, hbm],
        out_specs=(hbm, hbm, hbm),
        scratch_shapes=[
            pltpu.VMEM((cl, points), bf),
            pltpu.VMEM((v, points), bf),
            pltpu.VMEM((batch, points), f32),
            pltpu.VMEM((batch, cl, v), bf),
            pltpu.VMEM((batch * v, cl), bf),
            pltpu.VMEM((n, rows, cl), bf),
            pltpu.VMEM((q, planes, rows, v), bf),
            pltpu.VMEM((2, rows, points), bf),
            pltpu.VMEM((chips, 2, half, 2 * rows), f32),
            pltpu.VMEM((n, half, 2 * rows), f32),
            pltpu.VMEM((half, 2 * rows), bf),
            pltpu.VMEM((chips, half, 2 * rows), bf),
            pltpu.VMEM((half, 2 * rows), bf),
            pltpu.VMEM((n, half, 2 * rows), bf),
            dma, dma((2,)), dma((chips, 2)), dma,
            dma((n,)), dma((n,)), dma, dma, dma((planes,)), dma((planes,)), dma((q,)), dma((q,)),
            dma((chips, 2)), dma((n,)), dma((chips,)), dma((chips,)), dma((n,)), dma((n,)),
        ],
        compiler_params=pltpu.CompilerParams(
            collective_id=0, has_side_effects=True, vmem_limit_bytes=63 * 1024 * 1024
        ),
        name="gather_field",
    )(excitations, valence_orb, conduction_orb, screened)
    return pl.pallas_call(
        project_kernel,
        out_shape=jax.ShapeDtypeStruct((batch, cl, v), bf),
        in_specs=[hbm, hbm, hbm],
        out_specs=hbm,
        scratch_shapes=[
            pltpu.VMEM((cl, points), bf), pltpu.VMEM((v, points), bf), pltpu.VMEM((batch, points), f32),
            pltpu.VMEM((batch, cl, v), bf), dma((3,)), dma((batch // 2,))],
        compiler_params=pltpu.CompilerParams(vmem_limit_bytes=63 * 1024 * 1024),
        name="project",
    )(condt, valt, field)


def over_blocks(total_rows, step_fn, initial):
    span_size = math.gcd(total_rows, 2048)
    block_count = total_rows // span_size
    if block_count == 1:
        return step_fn(initial, 0, span_size)
    return lax.fori_loop(
        0, block_count, lambda index, carry: step_fn(carry, index * span_size, span_size), initial
    )


def density_rows(flat_exc, batch, valence_rows, cond_rows):
    total_rows = valence_rows.shape[0]
    cond_local = cond_rows.shape[1]
    initial = jnp.zeros((batch, total_rows), jnp.float32)

    def step_fn(carry, offset, span_size):
        val_block = lax.dynamic_slice_in_dim(valence_rows, offset, span_size, 0)
        cond_block = lax.dynamic_slice_in_dim(cond_rows, offset, span_size, 0)
        mixed = lax.dot_general(
            flat_exc, val_block, (((1,), (1,)), ((), ())), preferred_element_type=jnp.float32
        )
        mixed = mixed.reshape(batch, cond_local, span_size)
        summed = jnp.sum(mixed * cond_block.T.astype(jnp.float32)[None], axis=1)
        return lax.dynamic_update_slice_in_dim(carry, summed, offset, 1)

    return over_blocks(total_rows, step_fn, initial)


def projection(carry, valence_rows, cond_rows, field_cols):
    total_rows = valence_rows.shape[0]
    batch = field_cols.shape[0]
    cond_local = cond_rows.shape[1]

    def step_fn(inner, offset, span_size):
        val_block = lax.dynamic_slice_in_dim(valence_rows, offset, span_size, 0)
        cond_block = lax.dynamic_slice_in_dim(cond_rows, offset, span_size, 0)
        field_block = lax.dynamic_slice_in_dim(field_cols, offset, span_size, 1)
        pair = (
            cond_block.T.astype(jnp.float32)[None] * field_block.astype(jnp.float32)[:, None, :]
        ).astype(jnp.bfloat16)
        pair = pair.reshape(batch * cond_local, span_size)
        return inner + jnp.dot(pair, val_block, preferred_element_type=jnp.float32)

    return over_blocks(total_rows, step_fn, carry)


def general_body(excitations, valence_orb, conduction_orb, screened):
    batch, cond_local, valence = excitations.shape
    flat_exc = excitations.reshape(batch * cond_local, valence)
    valence_whole = lax.all_gather(valence_orb, "row", axis=0, tiled=True)
    cond_rows = lax.all_to_all(conduction_orb, "row", split_axis=1, concat_axis=0, tiled=True)
    partial_density = density_rows(flat_exc, batch, valence_whole, cond_rows)
    density_whole = lax.psum(partial_density, "row").astype(jnp.bfloat16)
    field_mine = lax.dot_general(
        density_whole, screened, (((1,), (1,)), ((), ())), preferred_element_type=jnp.float32
    ).astype(jnp.bfloat16)
    initial = jnp.zeros((batch * cond_local, valence), jnp.float32)
    summed = projection(
        initial, valence_whole, cond_rows, lax.all_gather(field_mine, "row", axis=1, tiled=True)
    )
    return summed.reshape(batch, cond_local, valence).astype(jnp.bfloat16)


def body(n, excitations, valence_orb, conduction_orb, screened):
    batch, cl, v = excitations.shape
    rows = valence_orb.shape[0]
    fits = n in (8, 16) and cl % 128 == 0 and v == 128 and rows == 64 and batch == 16
    if fits:
        return fast_body(n, excitations, valence_orb, conduction_orb, screened)
    return general_body(excitations, valence_orb, conduction_orb, screened)


def solution(mesh):
    in_specs = (
        P("grp", "row", None),
        P(("grp", "row"), None),
        P(("grp", "row"), None),
        P(("grp", "row"), None),
    )
    out_specs = P("grp", "row", None)
    return jax.shard_map(
        functools.partial(body, mesh.shape["row"]),
        mesh=mesh, in_specs=in_specs, out_specs=out_specs, check_vma=False,
    )
```

```python
import functools
import math

import jax
import jax.numpy as jnp
from jax import lax
from jax.experimental import pallas as pl
from jax.experimental.pallas import tpu as pltpu
from jax.sharding import PartitionSpec as P

MESH = pl.DeviceIdType.MESH
NT = (((1,), (1,)), ((), ()))


def flip(index, other, bits):
    total = 0
    for bit in range(bits):
        a = (index // (1 << bit)) % 2
        b = (other // (1 << bit)) % 2
        total = total + (a + b - 2 * a * b) * (1 << bit)
    return total


def send_order(n, q):
    far = list(range(n - 1, n // 2 - 1, -1))
    near = [1] + [k for k in range(n // 2 - 1, 1, -1) if k // 2 != q // 4]
    near[3:3] = [k for k in range(n // 2 - 1, 1, -1) if k // 2 == q // 4]
    order = []
    while far or near:
        order += far[:2] + near[:3]
        far, near = far[2:], near[3:]
    return order


def work_order(n, q):
    seen, order = {0}, [0]
    for k in send_order(n, q):
        seen.add(k)
        if seen >= {k, k ^ 1} and k // 2 not in order:
            order.append(k // 2)
    return order


def gather_kernel(
    n, planes,
    exc_hbm, val_ref, cond_hbm, scr_ref,
    condt_hbm, valt_hbm, field_hbm,
    condt_ref, valt_ref, field_ref, exc, exct, cond_all, val_all, scr_chip, part, red, dens, dens_all, fld, fld_all,
    exc_sem, own_sem, out_sem, field_sem,
    cond_send, cond_recv, scr_send, scr_recv, va_send, va_recv, vb_send, vb_recv,
    part_send, part_recv, dens_send, dens_recv, fld_send, fld_recv,
):
    rows, cl = val_ref.shape[0], exc.shape[1]
    batch = exc.shape[0]
    half = batch // 2
    q = n // planes
    bits = n.bit_length() - 1
    chips = n // 2
    me = lax.axis_index("row")
    my_z, my_q = me // q, me % q
    chip, core = me // 2, me % 2

    exc_copy = pltpu.make_async_copy(exc_hbm, exc, exc_sem)
    exc_copy.start()
    own_val = pltpu.make_async_copy(val_ref, val_all.at[my_q, my_z], own_sem.at[0])
    own_val.start()
    own_scr = pltpu.make_async_copy(scr_ref, scr_chip.at[core], own_sem.at[1])
    own_scr.start()
    pltpu.make_async_copy(
        cond_hbm.at[:, pl.ds(pl.multiple_of(me * cl, cl), cl)], cond_all.at[me], cond_recv.at[me]
    ).start()

    barrier = pltpu.get_barrier_semaphore()
    for k in range(1, n):
        pl.semaphore_signal(barrier, inc=1, device_id={"row": flip(me, k, bits)}, device_id_type=MESH)
    pl.semaphore_wait(barrier, n - 1)

    def remote(src, dst, send, recv, to):
        return pltpu.make_async_remote_copy(
            src_ref=src, dst_ref=dst, send_sem=send, recv_sem=recv,
            device_id={"row": to}, device_id_type=MESH,
        )

    sent = []
    zbits, qbits = planes.bit_length() - 1, q.bit_length() - 1
    for k in range(planes - 1, 0, -1):
        to = flip(my_z, k, zbits) * q + my_q
        copy = remote(val_ref, val_all.at[my_q, my_z], va_send.at[k], va_recv.at[my_z], to)
        copy.start()
        sent.append(copy)
    for k in send_order(n, q):
        to = flip(me, k, bits)
        copy = remote(
            cond_hbm.at[:, pl.ds(pl.multiple_of(to * cl, cl), cl)], cond_all.at[me],
            cond_send.at[k], cond_recv.at[me], to,
        )
        copy.start()
        sent.append(copy)
    copy = remote(scr_ref, scr_chip.at[core], scr_send, scr_recv, chip * 2 + 1 - core)
    copy.start()
    sent.append(copy)

    exc_copy.wait()

    def turn(b, carry):
        exct[pl.ds(pl.multiple_of(b * 128, 128), 128), :] = exc[b].T
        return carry

    lax.fori_loop(0, batch, turn, 0)

    own_val.wait()
    for k in range(1, planes):
        z = flip(my_z, k, zbits)
        pltpu.make_async_copy(val_ref, val_all.at[my_q, z], va_recv.at[z]).wait()
    for k in range(1, q):
        to = my_z * q + flip(my_q, k, qbits)
        copy = remote(val_all.at[my_q], val_all.at[my_q], vb_send.at[k], vb_recv.at[my_q], to)
        copy.start()
        sent.append(copy)
    for k in range(1, q):
        other = flip(my_q, k, qbits)
        pltpu.make_async_copy(val_all.at[other], val_all.at[other], vb_recv.at[other]).wait()

    def group(step, carry):
        k = 0
        for at, value in enumerate(work_order(n, q)):
            k = k + jnp.where(step == at, value, 0)
        p = flip(chip, k, bits - 1)
        z, y = p // (q // 2), p % (q // 2)
        lanes = pl.ds(pl.multiple_of(p * 2 * rows, 2 * rows), 2 * rows)
        for h in range(2):
            pltpu.make_async_copy(cond_all.at[2 * p + h], cond_all.at[2 * p + h], cond_recv.at[2 * p + h]).wait()
        block = cond_all[pl.ds(2 * p, 2)].reshape(2 * rows, cl)
        vals = jnp.concatenate([val_all[2 * y, z], val_all[2 * y + 1, z]], axis=0)
        valt = vals.astype(jnp.float32).T
        valt_ref[:, lanes] = valt.astype(jnp.bfloat16)
        mixed = lax.dot_general(exct[...], block, NT, preferred_element_type=jnp.float32)
        summed = jnp.sum(mixed.reshape(batch, valt.shape[0], 2 * rows) * valt[None], axis=1)
        part[k, 0] = summed[:half]
        part[k, 1] = summed[half:]

        @pl.when(k == 0)
        def _():
            remote(
                part.at[k, 1 - core], red.at[me], part_send.at[k, 1 - core], part_recv.at[me],
                2 * chip + 1 - core,
            ).start()
            red[me] = part[0, core]

        @pl.when(k > 0)
        def _():
            for h in range(2):
                remote(
                    part.at[k, h], red.at[me], part_send.at[k, h], part_recv.at[me], 2 * p + h
                ).start()

        condt_ref[:, lanes] = block.T
        pltpu.make_async_copy(condt_ref.at[:, lanes], condt_hbm.at[:, lanes], out_sem.at[k, 0]).start()
        pltpu.make_async_copy(valt_ref.at[:, lanes], valt_hbm.at[:, lanes], out_sem.at[k, 1]).start()
        return carry

    lax.fori_loop(0, chips, group, 0)

    own_scr.wait()
    pltpu.make_async_copy(scr_chip.at[1 - core], scr_chip.at[1 - core], scr_recv).wait()
    total = red[me]
    for k in range(1, n):
        other = flip(me, k, bits)
        pltpu.make_async_copy(red.at[other], red.at[other], part_recv.at[other]).wait()
        total = total + red[other]
    dens[...] = total.astype(jnp.bfloat16)
    dens_all[chip] = total.astype(jnp.bfloat16)
    for k in range(chips - 1, 0, -1):
        to = flip(chip, k, bits - 1)
        copy = remote(dens, dens_all.at[chip], dens_send.at[k], dens_recv.at[chip], 2 * to + core)
        copy.start()
        sent.append(copy)
    for k in range(1, chips):
        other = flip(chip, k, bits - 1)
        pltpu.make_async_copy(dens_all.at[other], dens_all.at[other], dens_recv.at[other]).wait()
    whole = jnp.concatenate([dens_all[p].astype(jnp.float32) for p in range(chips)], axis=1).astype(jnp.bfloat16)
    screened = scr_chip[...].reshape(2 * rows, scr_ref.shape[1])
    mine = lax.dot_general(whole, screened, NT, preferred_element_type=jnp.float32).astype(jnp.bfloat16)
    fld[...] = mine
    fld_all[me] = mine
    for k in range(n - 1, 0, -1):
        copy = remote(fld, fld_all.at[me], fld_send.at[k], fld_recv.at[me], flip(me, k, bits))
        copy.start()
        sent.append(copy)
    for k in range(1, n):
        other = flip(me, k, bits)
        pltpu.make_async_copy(fld_all.at[other], fld_all.at[other], fld_recv.at[other]).wait()
    for p in range(chips):
        for h in range(2):
            field_ref[h * half:(h + 1) * half, p * 2 * rows:(p + 1) * 2 * rows] = fld_all[2 * p + h].astype(jnp.float32)

    field_copy = pltpu.make_async_copy(field_ref, field_hbm, field_sem)
    field_copy.start()
    for k in range(chips):
        lanes = pl.ds(pl.multiple_of(flip(chip, k, bits - 1) * 2 * rows, 2 * rows), 2 * rows)
        pltpu.make_async_copy(condt_ref.at[:, lanes], condt_hbm.at[:, lanes], out_sem.at[k, 0]).wait()
        pltpu.make_async_copy(valt_ref.at[:, lanes], valt_hbm.at[:, lanes], out_sem.at[k, 1]).wait()
    for copy in sent:
        copy.wait_send()
    remote(
        part.at[0, 1 - core], red.at[me], part_send.at[0, 1 - core], part_recv.at[me], 2 * chip + 1 - core
    ).wait_send()
    for k in range(1, chips):
        p = flip(chip, k, bits - 1)
        for h in range(2):
            remote(part.at[k, h], red.at[me], part_send.at[k, h], part_recv.at[me], 2 * p + h).wait_send()
    field_copy.wait()


def project_kernel(condt_hbm, valt_hbm, field_hbm, out_hbm, condt_ref, valt_ref, field_ref, held, in_sem, out_sem):
    loads = [
        pltpu.make_async_copy(src, dst, in_sem.at[at])
        for at, (src, dst) in enumerate(((valt_hbm, valt_ref), (field_hbm, field_ref), (condt_hbm, condt_ref)))
    ]
    for load in loads:
        load.start()
    loads[0].wait()
    loads[1].wait()
    v = valt_ref.shape[0]
    batch = field_ref.shape[0]
    valt = valt_ref[...]
    copies = []
    for b in range(0, batch, 4):
        weights = jnp.concatenate(
            [valt * field_ref[b + i:b + i + 1, :].astype(jnp.bfloat16) for i in range(4)], axis=0
        )
        if b == 0:
            loads[2].wait()
        summed = lax.dot_general(condt_ref[...], weights, NT, preferred_element_type=jnp.float32)
        for i in range(4):
            held[b + i] = summed[:, i * v:(i + 1) * v].astype(jnp.bfloat16)
        copy = pltpu.make_async_copy(held.at[pl.ds(b, 4)], out_hbm.at[pl.ds(b, 4)], out_sem.at[b // 4])
        copy.start()
        copies.append(copy)
    for copy in copies:
        copy.wait()


def fast_body(n, excitations, valence_orb, conduction_orb, screened):
    batch, cl, v = excitations.shape
    rows, points = screened.shape
    planes = 4 if n % 8 == 0 else 2
    q, chips, half = n // planes, n // 2, batch // 2
    bf, f32 = jnp.bfloat16, jnp.float32
    hbm = pl.BlockSpec(memory_space=pltpu.HBM)
    dma = pltpu.SemaphoreType.DMA
    condt, valt, field = pl.pallas_call(
        functools.partial(gather_kernel, n, planes),
        out_shape=(
            jax.ShapeDtypeStruct((cl, points), bf),
            jax.ShapeDtypeStruct((v, points), bf),
            jax.ShapeDtypeStruct((batch, points), f32),
        ),
        in_specs=[hbm, hbm, hbm, hbm],
        out_specs=(hbm, hbm, hbm),
        scratch_shapes=[
            pltpu.VMEM((cl, points), bf),
            pltpu.VMEM((v, points), bf),
            pltpu.VMEM((batch, points), f32),
            pltpu.VMEM((batch, cl, v), bf),
            pltpu.VMEM((batch * v, cl), bf),
            pltpu.VMEM((n, rows, cl), bf),
            pltpu.VMEM((q, planes, rows, v), bf),
            pltpu.VMEM((2, rows, points), bf),
            pltpu.VMEM((chips, 2, half, 2 * rows), f32),
            pltpu.VMEM((n, half, 2 * rows), f32),
            pltpu.VMEM((half, 2 * rows), bf),
            pltpu.VMEM((chips, half, 2 * rows), bf),
            pltpu.VMEM((half, 2 * rows), bf),
            pltpu.VMEM((n, half, 2 * rows), bf),
            dma, dma((2,)), dma((chips, 2)), dma,
            dma((n,)), dma((n,)), dma, dma, dma((planes,)), dma((planes,)), dma((q,)), dma((q,)),
            dma((chips, 2)), dma((n,)), dma((chips,)), dma((chips,)), dma((n,)), dma((n,)),
        ],
        compiler_params=pltpu.CompilerParams(
            collective_id=0, has_side_effects=True, vmem_limit_bytes=63 * 1024 * 1024
        ),
        name="gather_field",
    )(excitations, valence_orb, conduction_orb, screened)
    return pl.pallas_call(
        project_kernel,
        out_shape=jax.ShapeDtypeStruct((batch, cl, v), bf),
        in_specs=[hbm, hbm, hbm],
        out_specs=hbm,
        scratch_shapes=[
            pltpu.VMEM((cl, points), bf), pltpu.VMEM((v, points), bf), pltpu.VMEM((batch, points), f32),
            pltpu.VMEM((batch, cl, v), bf), dma((3,)), dma((batch // 2,))],
        compiler_params=pltpu.CompilerParams(vmem_limit_bytes=63 * 1024 * 1024),
        name="project",
    )(condt, valt, field)


def over_blocks(total_rows, step_fn, initial):
    span_size = math.gcd(total_rows, 2048)
    block_count = total_rows // span_size
    if block_count == 1:
        return step_fn(initial, 0, span_size)
    return lax.fori_loop(
        0, block_count, lambda index, carry: step_fn(carry, index * span_size, span_size), initial
    )


def density_rows(flat_exc, batch, valence_rows, cond_rows):
    total_rows = valence_rows.shape[0]
    cond_local = cond_rows.shape[1]
    initial = jnp.zeros((batch, total_rows), jnp.float32)

    def step_fn(carry, offset, span_size):
        val_block = lax.dynamic_slice_in_dim(valence_rows, offset, span_size, 0)
        cond_block = lax.dynamic_slice_in_dim(cond_rows, offset, span_size, 0)
        mixed = lax.dot_general(
            flat_exc, val_block, (((1,), (1,)), ((), ())), preferred_element_type=jnp.float32
        )
        mixed = mixed.reshape(batch, cond_local, span_size)
        summed = jnp.sum(mixed * cond_block.T.astype(jnp.float32)[None], axis=1)
        return lax.dynamic_update_slice_in_dim(carry, summed, offset, 1)

    return over_blocks(total_rows, step_fn, initial)


def projection(carry, valence_rows, cond_rows, field_cols):
    total_rows = valence_rows.shape[0]
    batch = field_cols.shape[0]
    cond_local = cond_rows.shape[1]

    def step_fn(inner, offset, span_size):
        val_block = lax.dynamic_slice_in_dim(valence_rows, offset, span_size, 0)
        cond_block = lax.dynamic_slice_in_dim(cond_rows, offset, span_size, 0)
        field_block = lax.dynamic_slice_in_dim(field_cols, offset, span_size, 1)
        pair = (
            cond_block.T.astype(jnp.float32)[None] * field_block.astype(jnp.float32)[:, None, :]
        ).astype(jnp.bfloat16)
        pair = pair.reshape(batch * cond_local, span_size)
        return inner + jnp.dot(pair, val_block, preferred_element_type=jnp.float32)

    return over_blocks(total_rows, step_fn, carry)


def general_body(excitations, valence_orb, conduction_orb, screened):
    batch, cond_local, valence = excitations.shape
    flat_exc = excitations.reshape(batch * cond_local, valence)
    valence_whole = lax.all_gather(valence_orb, "row", axis=0, tiled=True)
    cond_rows = lax.all_to_all(conduction_orb, "row", split_axis=1, concat_axis=0, tiled=True)
    partial_density = density_rows(flat_exc, batch, valence_whole, cond_rows)
    density_whole = lax.psum(partial_density, "row").astype(jnp.bfloat16)
    field_mine = lax.dot_general(
        density_whole, screened, (((1,), (1,)), ((), ())), preferred_element_type=jnp.float32
    ).astype(jnp.bfloat16)
    initial = jnp.zeros((batch * cond_local, valence), jnp.float32)
    summed = projection(
        initial, valence_whole, cond_rows, lax.all_gather(field_mine, "row", axis=1, tiled=True)
    )
    return summed.reshape(batch, cond_local, valence).astype(jnp.bfloat16)


def body(n, excitations, valence_orb, conduction_orb, screened):
    batch, cl, v = excitations.shape
    rows = valence_orb.shape[0]
    fits = n in (8, 16) and cl % 128 == 0 and v == 128 and rows == 64 and batch == 16
    if fits:
        return fast_body(n, excitations, valence_orb, conduction_orb, screened)
    return general_body(excitations, valence_orb, conduction_orb, screened)


def solution(mesh):
    in_specs = (
        P("grp", "row", None),
        P(("grp", "row"), None),
        P(("grp", "row"), None),
        P(("grp", "row"), None),
    )
    out_specs = P("grp", "row", None)
    return jax.shard_map(
        functools.partial(body, mesh.shape["row"]),
        mesh=mesh, in_specs=in_specs, out_specs=out_specs, check_vma=False,
    )
```
